32 devices in a mesh: box: 2 (over core), row: 16 (over z, y, x).
Axes of the slice: x: 2, y: 2, z: 4, core: 2. Of those that a mesh axis runs over, the one named last changes fastest.
Arguments:
- dtn: float32 [4, 6, 384, 2304], P('box', None, 'row'), may hold values from -2 to 8, as said below
- interface_perm: int32 [2, 384], P('box'), may hold values from 0 to 383, each once within a row
Outputs:
- solution_first: float32 [2, 384, 3840], P('box', 'row')
- solution_second: float32 [2, 384, 6144], P('box', 'row')
- merged_map: float32 [2, 8, 384, 6144], P('box', None, 'row')
The draws below stay inside these ranges and needn't reach their ends.
Inputs may be any that keep to these rules, and one draw needn't show every extreme that they name: `dtn`: each box's map, read as a (2304) x (2304) matrix, is symmetric and positive definite.
All inputs are finite; a program needn't handle non-finite values.
Results may differ from the reference program's by a relative error of at most 0.00012.
Values sent between devices are 32-bit elements; how exact they have to be, the bound alone decides.
A program may use at most 192 MiB of HBM per device.

```python
import jax
import jax.numpy as jnp
from jax import lax

F = 384
NBOX = 4
NPAIR = 2


def one_map(key):
    order = 6 * F
    key_noise, key_scale = jax.random.split(key, 2)
    base_noise = jax.random.normal(key_noise, (order, order), jnp.float32)
    row_scale = 1.0 + 0.0 * jax.random.uniform(key_scale, (order,), jnp.float32)
    gram_matrix = jnp.dot(base_noise, base_noise.T, precision=lax.Precision.HIGHEST) / order
    gram_matrix = (gram_matrix + gram_matrix.T) * 0.5
    shifted = gram_matrix + 0.1 * jnp.eye(order, dtype=jnp.float32)
    scaled = row_scale[:, None] * shifted * row_scale[None, :]
    return scaled.reshape(6, F, order)


def draw_dtn(key, part):
    keys = jax.random.split(jax.random.fold_in(key, 11), NBOX)
    return jax.lax.map(one_map, keys)


def setup_inputs(seed: int = 0) -> dict:
    seeds = jax.random.split(jax.random.key(seed), 3)
    return {
        "dtn": draw_dtn(jax.random.fold_in(seeds[2], 71), 0),
        "interface_perm": jax.vmap(lambda own: jax.random.permutation(own, F))(jax.random.split(seeds[1], NPAIR)).reshape((NPAIR, F)).astype(jnp.int32),
    }


def face_index(faces, width):
    return jnp.concatenate([jnp.arange(width, dtype=jnp.int32) + f * width for f in faces])

def pick(matrix, rows, cols):
    return jnp.take(jnp.take(matrix, rows, axis=0), cols, axis=1)

def merge(left, right, left_s, left_o, right_s, right_o):
    couple = pick(left, left_s, left_s) + pick(right, right_s, right_s)
    coupled = jnp.concatenate([pick(left, left_s, left_o), pick(right, right_s, right_o)], axis=1)
    factor = jnp.linalg.cholesky(couple)
    solution = -jax.scipy.linalg.cho_solve((factor, True), coupled)
    n_left = left_o.shape[0]
    n_right = right_o.shape[0]
    top = jnp.concatenate([pick(left, left_o, left_o), jnp.zeros((n_left, n_right), jnp.float32)], axis=1)
    bottom = jnp.concatenate([jnp.zeros((n_right, n_left), jnp.float32), pick(right, right_o, right_o)], axis=1)
    lift = jnp.concatenate([pick(left, left_o, left_s), pick(right, right_o, right_s)], axis=0)
    merged = jnp.concatenate([top, bottom], axis=0) + jnp.dot(lift, solution, precision=lax.Precision.HIGHEST)
    return (solution, merged)

def reference(dtn, interface_perm):
    size = 6 * F
    firsts = []
    merged_one = []
    for p in range(NPAIR):
        first = dtn[2 * p].reshape(size, size)
        second = dtn[2 * p + 1].reshape(size, size)
        order = jnp.concatenate([interface_perm[p].astype(jnp.int32), jnp.arange(F, size, dtype=jnp.int32)])
        second = pick(second, order, order)
        solution, merged = merge(first, second, face_index([1], F), face_index([0, 2, 3, 4, 5], F), face_index([0], F), face_index([1, 2, 3, 4, 5], F))
        firsts.append(solution)
        merged_one.append(merged)
    seconds = []
    maps = []
    for c in range(NPAIR // 2):
        solution, merged = merge(merged_one[2 * c], merged_one[2 * c + 1], face_index([2, 7], F), face_index([0, 1, 3, 4, 5, 6, 8, 9], F), face_index([1, 6], F), face_index([0, 2, 3, 4, 5, 7, 8, 9], F))
        for h in range(2):
            seconds.append(solution[h * F:(h + 1) * F])
            maps.append(merged[h * 8 * F:(h + 1) * 8 * F].reshape(8, F, 16 * F))
    return (jnp.stack(firsts), jnp.stack(seconds), jnp.stack(maps))
```

```python
import functools

import jax
import jax.numpy as jnp
from jax import lax
from jax.experimental import pallas as pl
from jax.experimental.pallas import tpu as pltpu
from jax.sharding import PartitionSpec as P

HIGHEST = lax.Precision.HIGHEST
HIGH = lax.Precision.HIGH
BLOCK = 128
GROUP = 4


def dot(left, right, precision=HIGHEST):
    return jnp.dot(left, right, precision=precision, preferred_element_type=jnp.float32)


def dot_t(left, right):
    return lax.dot_general(
        left, right, (((0,), (0,)), ((), ())), precision=HIGHEST, preferred_element_type=jnp.float32
    )


def invert_block(blk):
    size = blk.shape[0]
    lane = lax.broadcasted_iota(jnp.int32, (1, size), 1)

    def step(g, carry):
        k = g * GROUP
        full = blk[...]
        cols = [
            jnp.take_along_axis(full, jnp.full((size, size), k + i, jnp.int32), axis=1)
            for i in range(GROUP)
        ]
        rows = [blk[pl.ds(k + i, 1), :] for i in range(GROUP)]
        wide = [jnp.broadcast_to(r, (8, size)) for r in rows]
        pivots = [
            [
                jnp.take_along_axis(wide[i], jnp.full((8, size), k + j, jnp.int32), axis=1)
                for j in range(GROUP)
            ]
            for i in range(GROUP)
        ]
        inside = (lane >= k) & (lane < k + GROUP)
        wide = [
            jnp.where(lane == k + i, 1.0, jnp.where(inside, 0.0, wide[i])) for i in range(GROUP)
        ]
        for i in range(GROUP):
            p = 1.0 / pivots[i][i]
            wide[i] = wide[i] * p
            for j in range(i + 1, GROUP):
                pivots[i][j] = pivots[i][j] * p
            for l in range(GROUP):
                if l != i:
                    f = pivots[l][i]
                    wide[l] = wide[l] - f * wide[i]
                    for j in range(i + 1, GROUP):
                        pivots[l][j] = pivots[l][j] - f * pivots[i][j]
        result = jnp.where(inside, 0.0, full)
        for i in range(GROUP):
            result = result - cols[i] * wide[i][0:1]
        blk[...] = result
        for i in range(GROUP):
            blk[pl.ds(k + i, 1), :] = wide[i][0:1]
        return carry

    lax.fori_loop(0, size // GROUP, step, 0)


def invert(mat, blk, col):
    order = mat.shape[0]
    count = order // BLOCK
    eye = (
        lax.broadcasted_iota(jnp.int32, (BLOCK, BLOCK), 0)
        == lax.broadcasted_iota(jnp.int32, (BLOCK, BLOCK), 1)
    ).astype(jnp.float32)

    def outer(j, carry):
        here = pl.ds(pl.multiple_of(j * BLOCK, BLOCK), BLOCK)
        blk[...] = mat[here, here]
        invert_block(blk)
        col[...] = mat[:, here]
        mat[:, here] = jnp.zeros((order, BLOCK), jnp.float32)
        mat[here, here] = eye
        col[here, :] = jnp.zeros((BLOCK, BLOCK), jnp.float32)
        mat[here, :] = dot(blk[...], mat[here, :])

        def inner(i, c):
            there = pl.ds(pl.multiple_of(i * BLOCK, BLOCK), BLOCK)
            mat[there, :] = mat[there, :] - dot(col[there, :], mat[here, :])
            return c

        @pl.loop(0, count)
        def _(i):
            @pl.when(i != j)
            def _():
                inner(i, 0)

        return carry

    lax.fori_loop(0, count, outer, 0)


def first_kernel(perm_ref, pair_ref, out_ref, mat, blk, col):
    f = mat.shape[0]
    place = (perm_ref[...] == lax.broadcasted_iota(jnp.int32, (f, f), 1)).astype(jnp.float32)
    moved = dot(place, pair_ref[:, f:])
    mat[...] = pair_ref[:, :f] + lax.dot_general(
        moved, place, (((1,), (1,)), ((), ())), precision=HIGHEST, preferred_element_type=jnp.float32
    )
    invert(mat, blk, col)
    inverse = mat[...]
    right = dot(inverse, place)
    out_ref[:f, :f] = inverse
    out_ref[:f, f:] = right
    out_ref[f:, :f] = dot_t(place, inverse)
    out_ref[f:, f:] = dot_t(place, right)


def second_kernel(own_ref, part_ref, lift_ref, pick_ref, out_ref, mat, blk, col):
    mat[...] = own_ref[...] + part_ref[...]
    invert(mat, blk, col)
    n = lift_ref.shape[0]
    out_ref[:n, :] = dot(lift_ref[...], mat[...])
    out_ref[n:, :] = dot(pick_ref[...], mat[...])


def call(kernel, out, order, *args):
    return pl.pallas_call(
        kernel,
        out_shape=jax.ShapeDtypeStruct(out, jnp.float32),
        in_specs=[pl.BlockSpec(memory_space=pltpu.VMEM)] * len(args),
        out_specs=pl.BlockSpec(memory_space=pltpu.VMEM),
        scratch_shapes=[
            pltpu.VMEM((order, order), jnp.float32),
            pltpu.VMEM((BLOCK, BLOCK), jnp.float32),
            pltpu.VMEM((order, BLOCK), jnp.float32),
        ],
        compiler_params=pltpu.CompilerParams(vmem_limit_bytes=40 * 1024 * 1024),
        cost_estimate=pl.CostEstimate(
            flops=order * 200_000_000, bytes_accessed=order * order * 8, transcendentals=0
        ),
    )(*args)


def body(dtn, interface_perm):
    a, b = dtn[0], dtn[1]
    count = a.shape[1]
    f = a.shape[2] // 6
    perm = interface_perm[0]
    rank = lax.axis_index("row")
    half = lax.axis_index("box") % 2
    first = half == 0

    def swap(x):
        n = lax.axis_size("box")
        return lax.ppermute(x, "box", [(i, i ^ 1) for i in range(n)])

    def gather(x):
        return lax.all_gather(x, "row", axis=0, tiled=True)

    def cols(x, face):
        return x[..., face * f : (face + 1) * f]

    def side(x):
        return jnp.where(first, cols(x, 3), cols(x, 2))

    def free(x):
        return jnp.where(first, cols(x, 2), cols(x, 3))

    def outer_cols(x, edge):
        return jnp.concatenate([cols(x, edge), free(x), cols(x, 4), cols(x, 5)], axis=-1)

    ay, by = jnp.where(first, a[3], a[2]), jnp.where(first, b[3], b[2])
    a1, b0 = a[1], b[0]
    pair = gather(jnp.concatenate([cols(a1, 1), cols(b0, 0)], axis=1))
    mid = gather(jnp.concatenate([side(a1), side(b0), side(ay), side(by)], axis=1))
    bulk_local = jnp.concatenate(
        [outer_cols(a1, 0), outer_cols(ay, 0), outer_cols(b0, 1), outer_cols(by, 1)], axis=1
    )
    bulk_local, _ = lax.optimization_barrier((bulk_local, mid[:8, :128]))
    bulk = gather(bulk_local)

    inv1 = call(first_kernel, (2 * f, 2 * f), f, perm[:, None], pair)
    a1y, b0y, ayy, byy = (mid[:, i * f : (i + 1) * f] for i in range(4))
    coupled = -jnp.concatenate([dot_t(a1y, inv1[:f]), dot_t(b0y, inv1[f:])], axis=0)

    def times_side(x):
        return jnp.concatenate([dot(x[:, :f], a1y), dot(x[:, f:], b0y)], axis=1)

    zero = jnp.zeros((f, f), jnp.float32)
    own_ss = times_side(coupled) + jnp.concatenate(
        [jnp.concatenate([ayy, zero], axis=1), jnp.concatenate([zero, byy], axis=1)], axis=0
    )
    part_ss = swap(own_ss)
    outer_a = jnp.concatenate(
        [a[0], jnp.where(first, a[2], a[3]), a[4], a[5]], axis=0
    )
    outer_b = jnp.concatenate(
        [b[1], jnp.where(first, b[2], b[3]), b[4], b[5]], axis=0
    )
    lift = -jnp.concatenate(
        [dot(cols(outer_a, 1), inv1[:f]), dot(cols(outer_b, 0), inv1[f:])], axis=0
    )
    n = 4 * count
    zero_n = jnp.zeros((n, f), jnp.float32)
    lift_two = times_side(lift) + jnp.concatenate(
        [
            jnp.concatenate([side(outer_a), zero_n], axis=1),
            jnp.concatenate([zero_n, side(outer_b)], axis=1),
        ],
        axis=0,
    )
    start = rank * count
    pick = (
        jnp.arange(2 * f, dtype=jnp.int32)[None, :]
        == half * f + start + jnp.arange(count, dtype=jnp.int32)[:, None]
    ).astype(jnp.float32)
    own_rows = lax.dynamic_slice(inv1, (start, 0), (count, 2 * f))
    z = -call(second_kernel, (2 * n + count, 2 * f), 2 * f, own_ss, part_ss, lift_two, pick)
    z_part = swap(z)
    both = jnp.concatenate([z_part, z], axis=0)
    through = dot(both, coupled)
    m = 2 * n + count
    through = jnp.concatenate(
        [through[:m], through[m : m + 2 * n] + lift, through[m + 2 * n :], -own_rows], axis=0
    )
    both = jnp.concatenate([both, jnp.zeros((count, 2 * f), jnp.float32)], axis=0)
    w = 4 * f
    res_a = dot(through[:, :f], bulk[:, :w], HIGH) + dot(both[:, :f], bulk[:, w : 2 * w], HIGH)
    res_b = dot(through[:, f:], bulk[:, 2 * w : 3 * w], HIGH) + dot(both[:, f:], bulk[:, 3 * w :], HIGH)
    results = jnp.concatenate([res_a, res_b], axis=1)
    cross = swap(results[:m])
    own = results[m : 2 * m]
    base = jnp.concatenate(
        [
            jnp.concatenate([outer_cols(outer_a, 0), jnp.zeros((n, w), jnp.float32)], axis=1),
            jnp.concatenate([jnp.zeros((n, w), jnp.float32), outer_cols(outer_b, 1)], axis=1),
        ],
        axis=0,
    )
    own_map = own[: 2 * n] + base
    left = jnp.where(first, own_map, cross[: 2 * n])
    right = jnp.where(first, cross[: 2 * n], own_map)
    merged_map = jnp.concatenate([left, right], axis=1).reshape(1, 8, count, 4 * w)
    own_s, cross_s = own[2 * n :], cross[2 * n :]
    second = jnp.concatenate(
        [jnp.where(first, own_s, cross_s), jnp.where(first, cross_s, own_s)], axis=1
    )
    s1 = results[2 * m :]
    y_a, y_b = -dot(own_rows[:, :f], a1y), -dot(own_rows[:, f:], b0y)

    def ordered(x, y):
        two = jnp.where(first, cols(x, 1), y)
        three = jnp.where(first, y, cols(x, 1))
        return [cols(x, 0), two, three, x[:, 2 * f :]]

    solution_first = jnp.concatenate(ordered(s1[:, :w], y_a) + ordered(s1[:, w:], y_b), axis=1)
    return (solution_first[None], second[None], merged_map)


def solution(mesh):
    return jax.shard_map(
        body,
        mesh=mesh,
        in_specs=(P("box", None, "row", None), P("box", None)),
        out_specs=(P("box", "row", None), P("box", "row", None), P("box", None, "row", None)),
        check_vma=False,
    )
```

```python
import functools

import jax
import jax.numpy as jnp
from jax import lax
from jax.experimental import pallas as pl
from jax.experimental.pallas import tpu as pltpu
from jax.sharding import PartitionSpec as P

HIGHEST = lax.Precision.HIGHEST
HIGH = lax.Precision.HIGH
BLOCK = 128
GROUP = 4


def dot(left, right, precision=HIGHEST):
    return jnp.dot(left, right, precision=precision, preferred_element_type=jnp.float32)


def dot_t(left, right):
    return lax.dot_general(
        left, right, (((0,), (0,)), ((), ())), precision=HIGHEST, preferred_element_type=jnp.float32
    )


def invert_block(blk):
    size = blk.shape[0]
    lane = lax.broadcasted_iota(jnp.int32, (1, size), 1)

    def step(g, carry):
        k = g * GROUP
        full = blk[...]
        cols = [
            jnp.take_along_axis(full, jnp.full((size, size), k + i, jnp.int32), axis=1)
            for i in range(GROUP)
        ]
        rows = [blk[pl.ds(k + i, 1), :] for i in range(GROUP)]
        wide = [jnp.broadcast_to(r, (8, size)) for r in rows]
        pivots = [
            [
                jnp.take_along_axis(wide[i], jnp.full((8, size), k + j, jnp.int32), axis=1)
                for j in range(GROUP)
            ]
            for i in range(GROUP)
        ]
        inside = (lane >= k) & (lane < k + GROUP)
        wide = [
            jnp.where(lane == k + i, 1.0, jnp.where(inside, 0.0, wide[i])) for i in range(GROUP)
        ]
        for i in range(GROUP):
            p = 1.0 / pivots[i][i]
            wide[i] = wide[i] * p
            for j in range(i + 1, GROUP):
                pivots[i][j] = pivots[i][j] * p
            for l in range(GROUP):
                if l != i:
                    f = pivots[l][i]
                    wide[l] = wide[l] - f * wide[i]
                    for j in range(i + 1, GROUP):
                        pivots[l][j] = pivots[l][j] - f * pivots[i][j]
        result = jnp.where(inside, 0.0, full)
        for i in range(GROUP):
            result = result - cols[i] * wide[i][0:1]
        blk[...] = result
        for i in range(GROUP):
            blk[pl.ds(k + i, 1), :] = wide[i][0:1]
        return carry

    lax.fori_loop(0, size // GROUP, step, 0)


def invert(mat, blk, col):
    order = mat.shape[0]
    count = order // BLOCK
    eye = (
        lax.broadcasted_iota(jnp.int32, (BLOCK, BLOCK), 0)
        == lax.broadcasted_iota(jnp.int32, (BLOCK, BLOCK), 1)
    ).astype(jnp.float32)

    def outer(j, carry):
        here = pl.ds(pl.multiple_of(j * BLOCK, BLOCK), BLOCK)
        blk[...] = mat[here, here]
        invert_block(blk)
        col[...] = mat[:, here]
        mat[:, here] = jnp.zeros((order, BLOCK), jnp.float32)
        mat[here, here] = eye
        col[here, :] = jnp.zeros((BLOCK, BLOCK), jnp.float32)
        mat[here, :] = dot(blk[...], mat[here, :])

        def inner(i, c):
            there = pl.ds(pl.multiple_of(i * BLOCK, BLOCK), BLOCK)
            mat[there, :] = mat[there, :] - dot(col[there, :], mat[here, :])
            return c

        @pl.loop(0, count)
        def _(i):
            @pl.when(i != j)
            def _():
                inner(i, 0)

        return carry

    lax.fori_loop(0, count, outer, 0)


def first_kernel(perm_ref, small_ref, inv_ref, coupled_ref, own_ref, mat, blk, col):
    f = mat.shape[0]
    place = (perm_ref[...] == lax.broadcasted_iota(jnp.int32, (f, f), 1)).astype(jnp.float32)
    a11, b00, a1y, b0y, ayy, byy = (small_ref[:, i * f : (i + 1) * f] for i in range(6))
    moved = dot(place, b00)
    mat[...] = a11 + lax.dot_general(
        moved, place, (((1,), (1,)), ((), ())), precision=HIGHEST, preferred_element_type=jnp.float32
    )
    invert(mat, blk, col)
    inverse = mat[...]
    right = dot(inverse, place)
    inv_ref[:f, :f] = inverse
    inv_ref[:f, f:] = right
    inv_ref[f:, :f] = dot_t(place, inverse)
    inv_ref[f:, f:] = dot_t(place, right)
    for h, x, d in ((0, a1y, ayy), (1, b0y, byy)):
        here = pl.ds(h * f, f)
        coupled_ref[here, :] = -dot_t(x, inv_ref[here, :])
        own_ref[here, :f] = dot(coupled_ref[here, :f], a1y)
        own_ref[here, f:] = dot(coupled_ref[here, f:], b0y)
        own_ref[here, here] = own_ref[here, here] + d


def second_kernel(own_ref, part_ref, lift_ref, pick_ref, out_ref, mat, blk, col):
    mat[...] = own_ref[...] + part_ref[...]
    invert(mat, blk, col)
    n = lift_ref.shape[0]
    out_ref[:n, :] = dot(lift_ref[...], mat[...])
    out_ref[n:, :] = dot(pick_ref[...], mat[...])


def call(kernel, out, order, *args):
    return pl.pallas_call(
        kernel,
        out_shape=[jax.ShapeDtypeStruct(o, jnp.float32) for o in out],
        in_specs=[pl.BlockSpec(memory_space=pltpu.VMEM)] * len(args),
        out_specs=[pl.BlockSpec(memory_space=pltpu.VMEM)] * len(out),
        scratch_shapes=[
            pltpu.VMEM((order, order), jnp.float32),
            pltpu.VMEM((BLOCK, BLOCK), jnp.float32),
            pltpu.VMEM((order, BLOCK), jnp.float32),
        ],
        compiler_params=pltpu.CompilerParams(vmem_limit_bytes=40 * 1024 * 1024),
        cost_estimate=pl.CostEstimate(
            flops=order * 20_000_000, bytes_accessed=order * order * 8, transcendentals=0
        ),
    )(*args)


def body(dtn, interface_perm):
    a, b = dtn[0], dtn[1]
    count = a.shape[1]
    f = a.shape[2] // 6
    perm = interface_perm[0]
    rank = lax.axis_index("row")
    half = lax.axis_index("box") % 2
    first = half == 0

    def swap(x):
        n = lax.axis_size("box")
        return lax.ppermute(x, "box", [(i, i ^ 1) for i in range(n)])

    def gather(x):
        return lax.all_gather(x, "row", axis=0, tiled=True)

    def cols(x, face):
        return x[..., face * f : (face + 1) * f]

    def side(x):
        return jnp.where(first, cols(x, 3), cols(x, 2))

    def free(x):
        return jnp.where(first, cols(x, 2), cols(x, 3))

    def outer_cols(x, edge):
        return jnp.concatenate([cols(x, edge), free(x), cols(x, 4), cols(x, 5)], axis=-1)

    ay, by = jnp.where(first, a[3], a[2]), jnp.where(first, b[3], b[2])
    a1, b0 = a[1], b[0]
    small = gather(
        jnp.concatenate(
            [cols(a1, 1), cols(b0, 0), side(a1), side(b0), side(ay), side(by)], axis=1
        )
    )
    bulk = gather(
        jnp.concatenate(
            [outer_cols(a1, 0), outer_cols(ay, 0), outer_cols(b0, 1), outer_cols(by, 1)], axis=1
        )
    )
    inv1, coupled, own_ss = call(first_kernel, [(2 * f, 2 * f)] * 3, f, perm[:, None], small)
    a1y, b0y = small[:, 2 * f : 3 * f], small[:, 3 * f : 4 * f]

    def times_side(x):
        return jnp.concatenate([dot(x[:, :f], a1y), dot(x[:, f:], b0y)], axis=1)

    part_ss = swap(own_ss)
    outer_a = jnp.concatenate(
        [a[0], jnp.where(first, a[2], a[3]), a[4], a[5]], axis=0
    )
    outer_b = jnp.concatenate(
        [b[1], jnp.where(first, b[2], b[3]), b[4], b[5]], axis=0
    )
    lift = -jnp.concatenate(
        [dot(cols(outer_a, 1), inv1[:f]), dot(cols(outer_b, 0), inv1[f:])], axis=0
    )
    n = 4 * count
    zero_n = jnp.zeros((n, f), jnp.float32)
    lift_two = times_side(lift) + jnp.concatenate(
        [
            jnp.concatenate([side(outer_a), zero_n], axis=1),
            jnp.concatenate([zero_n, side(outer_b)], axis=1),
        ],
        axis=0,
    )
    start = rank * count
    pick = (
        jnp.arange(2 * f, dtype=jnp.int32)[None, :]
        == half * f + start + jnp.arange(count, dtype=jnp.int32)[:, None]
    ).astype(jnp.float32)
    own_rows = lax.dynamic_slice(inv1, (start, 0), (count, 2 * f))
    z = -call(second_kernel, [(2 * n + count, 2 * f)], 2 * f, own_ss, part_ss, lift_two, pick)[0]
    z_part = swap(z)
    both = jnp.concatenate([z_part, z], axis=0)
    through = dot(both, coupled)
    m = 2 * n + count
    through = jnp.concatenate(
        [through[:m], through[m : m + 2 * n] + lift, through[m + 2 * n :], -own_rows], axis=0
    )
    both = jnp.concatenate([both, jnp.zeros((count, 2 * f), jnp.float32)], axis=0)
    w = 4 * f
    res_a = dot(through[:, :f], bulk[:, :w], HIGH) + dot(both[:, :f], bulk[:, w : 2 * w], HIGH)
    res_b = dot(through[:, f:], bulk[:, 2 * w : 3 * w], HIGH) + dot(both[:, f:], bulk[:, 3 * w :], HIGH)
    results = jnp.concatenate([res_a, res_b], axis=1)
    cross = swap(results[:m])
    own = results[m : 2 * m]
    base = jnp.concatenate(
        [
            jnp.concatenate([outer_cols(outer_a, 0), jnp.zeros((n, w), jnp.float32)], axis=1),
            jnp.concatenate([jnp.zeros((n, w), jnp.float32), outer_cols(outer_b, 1)], axis=1),
        ],
        axis=0,
    )
    own_map = own[: 2 * n] + base
    left = jnp.where(first, own_map, cross[: 2 * n])
    right = jnp.where(first, cross[: 2 * n], own_map)
    merged_map = jnp.concatenate([left, right], axis=1).reshape(1, 8, count, 4 * w)
    own_s, cross_s = own[2 * n :], cross[2 * n :]
    second = jnp.concatenate(
        [jnp.where(first, own_s, cross_s), jnp.where(first, cross_s, own_s)], axis=1
    )
    s1 = results[2 * m :]
    y_a, y_b = -dot(own_rows[:, :f], a1y), -dot(own_rows[:, f:], b0y)

    def ordered(x, y):
        two = jnp.where(first, cols(x, 1), y)
        three = jnp.where(first, y, cols(x, 1))
        return [cols(x, 0), two, three, x[:, 2 * f :]]

    solution_first = jnp.concatenate(ordered(s1[:, :w], y_a) + ordered(s1[:, w:], y_b), axis=1)
    return (solution_first[None], second[None], merged_map)


def solution(mesh):
    return jax.shard_map(
        body,
        mesh=mesh,
        in_specs=(P("box", None, "row", None), P("box", None)),
        out_specs=(P("box", "row", None), P("box", "row", None), P("box", None, "row", None)),
        check_vma=False,
    )
```

```python
import functools

import jax
import jax.numpy as jnp
from jax import lax
from jax.experimental import pallas as pl
from jax.experimental.pallas import tpu as pltpu
from jax.sharding import PartitionSpec as P

HIGHEST = lax.Precision.HIGHEST
HIGH = lax.Precision.HIGH
BLOCK = 128
GROUP = 4


def dot(left, right, precision=HIGHEST):
    return jnp.dot(left, right, precision=precision, preferred_element_type=jnp.float32)


def dot_t(left, right):
    return lax.dot_general(
        left, right, (((0,), (0,)), ((), ())), precision=HIGHEST, preferred_element_type=jnp.float32
    )


def invert_block(blk):
    size = blk.shape[0]
    lane = lax.broadcasted_iota(jnp.int32, (1, size), 1)

    def step(g, carry):
        k = g * GROUP
        full = blk[...]
        cols = [
            jnp.take_along_axis(full, jnp.full((size, size), k + i, jnp.int32), axis=1)
            for i in range(GROUP)
        ]
        rows = [blk[pl.ds(k + i, 1), :] for i in range(GROUP)]
        wide = [jnp.broadcast_to(r, (8, size)) for r in rows]
        pivots = [
            [
                jnp.take_along_axis(wide[i], jnp.full((8, size), k + j, jnp.int32), axis=1)
                for j in range(GROUP)
            ]
            for i in range(GROUP)
        ]
        inside = (lane >= k) & (lane < k + GROUP)
        wide = [
            jnp.where(lane == k + i, 1.0, jnp.where(inside, 0.0, wide[i])) for i in range(GROUP)
        ]
        for i in range(GROUP):
            p = 1.0 / pivots[i][i]
            wide[i] = wide[i] * p
            for j in range(i + 1, GROUP):
                pivots[i][j] = pivots[i][j] * p
            for l in range(GROUP):
                if l != i:
                    f = pivots[l][i]
                    wide[l] = wide[l] - f * wide[i]
                    for j in range(i + 1, GROUP):
                        pivots[l][j] = pivots[l][j] - f * pivots[i][j]
        result = jnp.where(inside, 0.0, full)
        for i in range(GROUP):
            result = result - cols[i] * wide[i][0:1]
        blk[...] = result
        for i in range(GROUP):
            blk[pl.ds(k + i, 1), :] = wide[i][0:1]
        return carry

    lax.fori_loop(0, size // GROUP, step, 0)


def invert(mat, blk, col):
    order = mat.shape[0]
    count = order // BLOCK
    eye = (
        lax.broadcasted_iota(jnp.int32, (BLOCK, BLOCK), 0)
        == lax.broadcasted_iota(jnp.int32, (BLOCK, BLOCK), 1)
    ).astype(jnp.float32)

    def outer(j, carry):
        here = pl.ds(pl.multiple_of(j * BLOCK, BLOCK), BLOCK)
        blk[...] = mat[here, here]
        invert_block(blk)
        col[...] = mat[:, here]
        mat[:, here] = jnp.zeros((order, BLOCK), jnp.float32)
        mat[here, here] = eye
        col[here, :] = jnp.zeros((BLOCK, BLOCK), jnp.float32)
        mat[here, :] = dot(blk[...], mat[here, :])

        def inner(i, c):
            there = pl.ds(pl.multiple_of(i * BLOCK, BLOCK), BLOCK)
            mat[there, :] = mat[there, :] - dot(col[there, :], mat[here, :])
            return c

        @pl.loop(0, count)
        def _(i):
            @pl.when(i != j)
            def _():
                inner(i, 0)

        return carry

    lax.fori_loop(0, count, outer, 0)


def first_kernel(perm_ref, small_ref, inv_ref, coupled_ref, own_ref, mat, blk, col):
    f = mat.shape[0]
    place = (perm_ref[...] == lax.broadcasted_iota(jnp.int32, (f, f), 1)).astype(jnp.float32)
    a11, b00, a1y, b0y, ayy, byy = (small_ref[:, i * f : (i + 1) * f] for i in range(6))
    moved = dot(place, b00)
    mat[...] = a11 + lax.dot_general(
        moved, place, (((1,), (1,)), ((), ())), precision=HIGHEST, preferred_element_type=jnp.float32
    )
    invert(mat, blk, col)
    inverse = mat[...]
    right = dot(inverse, place)
    inv_ref[:f, :f] = inverse
    inv_ref[:f, f:] = right
    inv_ref[f:, :f] = dot_t(place, inverse)
    inv_ref[f:, f:] = dot_t(place, right)
    for h, x, d in ((0, a1y, ayy), (1, b0y, byy)):
        here = pl.ds(h * f, f)
        coupled_ref[here, :] = -dot_t(x, inv_ref[here, :])
        own_ref[here, :f] = dot(coupled_ref[here, :f], a1y)
        own_ref[here, f:] = dot(coupled_ref[here, f:], b0y)
        own_ref[here, here] = own_ref[here, here] + d


def second_kernel(own_ref, part_ref, lift_ref, pick_ref, out_ref, mat, blk, col):
    mat[...] = own_ref[...] + part_ref[...]
    invert(mat, blk, col)
    n = lift_ref.shape[0]
    out_ref[:n, :] = dot(lift_ref[...], mat[...])
    out_ref[n:, :] = dot(pick_ref[...], mat[...])


def flip(index, bit):
    return index + bit - 2 * bit * ((index // bit) % 2)


def plan(n, width):
    bits = []
    bit = n // 2
    while bit:
        bits.append(bit)
        bit //= 2
    tiles = width // 128
    first = tiles * 3 // 8
    second = tiles * 3 // 8 + (tiles * 3 % 8 >= 4)
    orders = [bits, bits[:-2] + [1, 2], [1, 2] + bits[:-2]]
    sizes = [first, second, tiles - first - second]
    chunks, at = [], 0
    for order, size in zip(orders, sizes):
        chunks.append((at * 128, size * 128, order))
        at += size
    return bits, chunks


def gather_kernel(n, bits, chunks, x_ref, out_ref, send_sem, recv_sem, own_sem):
    me = lax.axis_index("row")
    barrier = pltpu.get_barrier_semaphore()
    for bit in bits:
        pl.semaphore_signal(
            barrier, inc=1, device_id={"row": flip(me, bit)}, device_id_type=pl.DeviceIdType.MESH
        )
    local = pltpu.make_async_copy(x_ref, out_ref.at[me], own_sem)
    local.start()
    local.wait()
    pl.semaphore_wait(barrier, len(bits))
    pending = [[] for _ in chunks]
    sent = []
    held = [[()] for _ in chunks]
    for t in range(len(bits)):
        for c, (start, size, order) in enumerate(chunks):
            for copy in pending[c]:
                copy.wait_recv()
            pending[c] = []
            bit = order[t]
            for s in held[c]:
                slot = me
                for one in s:
                    slot = flip(slot, one)
                number = (1 << t) - 1 + len(pending[c])
                piece = out_ref.at[slot, :, pl.ds(start, size)]
                copy = pltpu.make_async_remote_copy(
                    src_ref=piece,
                    dst_ref=piece,
                    send_sem=send_sem.at[c, number],
                    recv_sem=recv_sem.at[c, number],
                    device_id={"row": flip(me, bit)},
                    device_id_type=pl.DeviceIdType.MESH,
                )
                copy.start()
                pending[c].append(copy)
                sent.append(copy)
            held[c] = held[c] + [s + (bit,) for s in held[c]]
    for c in range(len(chunks)):
        for copy in pending[c]:
            copy.wait_recv()
    for copy in sent:
        copy.wait_send()


def quick_gather(x):
    n = lax.axis_size("row")
    count, width = x.shape
    bits, chunks = plan(n, width)
    out = pl.pallas_call(
        functools.partial(gather_kernel, n, bits, chunks),
        out_shape=jax.ShapeDtypeStruct((n, count, width), jnp.float32),
        in_specs=[pl.BlockSpec(memory_space=pltpu.VMEM)],
        out_specs=pl.BlockSpec(memory_space=pltpu.VMEM),
        scratch_shapes=[
            pltpu.SemaphoreType.DMA((len(chunks), n - 1)),
            pltpu.SemaphoreType.DMA((len(chunks), n - 1)),
            pltpu.SemaphoreType.DMA,
        ],
        compiler_params=pltpu.CompilerParams(
            collective_id=0, has_side_effects=True, vmem_limit_bytes=16 * 1024 * 1024
        ),
        cost_estimate=pl.CostEstimate(
            flops=10_000_000_000, bytes_accessed=2 * n * count * width * 4, transcendentals=0
        ),
    )(x)
    return out.reshape(n * count, width)


def call(kernel, out, order, *args):
    return pl.pallas_call(
        kernel,
        out_shape=[jax.ShapeDtypeStruct(o, jnp.float32) for o in out],
        in_specs=[pl.BlockSpec(memory_space=pltpu.VMEM)] * len(args),
        out_specs=[pl.BlockSpec(memory_space=pltpu.VMEM)] * len(out),
        scratch_shapes=[
            pltpu.VMEM((order, order), jnp.float32),
            pltpu.VMEM((BLOCK, BLOCK), jnp.float32),
            pltpu.VMEM((order, BLOCK), jnp.float32),
        ],
        compiler_params=pltpu.CompilerParams(vmem_limit_bytes=40 * 1024 * 1024),
        cost_estimate=pl.CostEstimate(
            flops=order * 20_000_000, bytes_accessed=order * order * 8, transcendentals=0
        ),
    )(*args)


def body(dtn, interface_perm):
    a, b = dtn[0], dtn[1]
    count = a.shape[1]
    f = a.shape[2] // 6
    perm = interface_perm[0]
    rank = lax.axis_index("row")
    half = lax.axis_index("box") % 2
    first = half == 0

    def swap(x):
        n = lax.axis_size("box")
        return lax.ppermute(x, "box", [(i, i ^ 1) for i in range(n)])

    def gather(x):
        return lax.all_gather(x, "row", axis=0, tiled=True)

    def cols(x, face):
        return x[..., face * f : (face + 1) * f]

    def side(x):
        return jnp.where(first, cols(x, 3), cols(x, 2))

    def free(x):
        return jnp.where(first, cols(x, 2), cols(x, 3))

    def outer_cols(x, edge):
        return jnp.concatenate([cols(x, edge), free(x), cols(x, 4), cols(x, 5)], axis=-1)

    ay, by = jnp.where(first, a[3], a[2]), jnp.where(first, b[3], b[2])
    a1, b0 = a[1], b[0]
    small = quick_gather(
        jnp.concatenate(
            [cols(a1, 1), cols(b0, 0), side(a1), side(b0), side(ay), side(by)], axis=1
        )
    )
    bulk = gather(
        jnp.concatenate(
            [outer_cols(a1, 0), outer_cols(ay, 0), outer_cols(b0, 1), outer_cols(by, 1)], axis=1
        )
    )
    inv1, coupled, own_ss = call(first_kernel, [(2 * f, 2 * f)] * 3, f, perm[:, None], small)
    a1y, b0y = small[:, 2 * f : 3 * f], small[:, 3 * f : 4 * f]

    def times_side(x):
        return jnp.concatenate([dot(x[:, :f], a1y), dot(x[:, f:], b0y)], axis=1)

    part_ss = swap(own_ss)
    outer_a = jnp.concatenate(
        [a[0], jnp.where(first, a[2], a[3]), a[4], a[5]], axis=0
    )
    outer_b = jnp.concatenate(
        [b[1], jnp.where(first, b[2], b[3]), b[4], b[5]], axis=0
    )
    lift = -jnp.concatenate(
        [dot(cols(outer_a, 1), inv1[:f]), dot(cols(outer_b, 0), inv1[f:])], axis=0
    )
    n = 4 * count
    zero_n = jnp.zeros((n, f), jnp.float32)
    lift_two = times_side(lift) + jnp.concatenate(
        [
            jnp.concatenate([side(outer_a), zero_n], axis=1),
            jnp.concatenate([zero_n, side(outer_b)], axis=1),
        ],
        axis=0,
    )
    start = rank * count
    pick = (
        jnp.arange(2 * f, dtype=jnp.int32)[None, :]
        == half * f + start + jnp.arange(count, dtype=jnp.int32)[:, None]
    ).astype(jnp.float32)
    own_rows = lax.dynamic_slice(inv1, (start, 0), (count, 2 * f))
    z = -call(second_kernel, [(2 * n + count, 2 * f)], 2 * f, own_ss, part_ss, lift_two, pick)[0]
    z_part = swap(z)
    both = jnp.concatenate([z_part, z], axis=0)
    through = dot(both, coupled)
    m = 2 * n + count
    through = jnp.concatenate(
        [through[:m], through[m : m + 2 * n] + lift, through[m + 2 * n :], -own_rows], axis=0
    )
    both = jnp.concatenate([both, jnp.zeros((count, 2 * f), jnp.float32)], axis=0)
    w = 4 * f
    res_a = dot(through[:, :f], bulk[:, :w], HIGH) + dot(both[:, :f], bulk[:, w : 2 * w], HIGH)
    res_b = dot(through[:, f:], bulk[:, 2 * w : 3 * w], HIGH) + dot(both[:, f:], bulk[:, 3 * w :], HIGH)
    results = jnp.concatenate([res_a, res_b], axis=1)
    cross = swap(results[:m])
    own = results[m : 2 * m]
    base = jnp.concatenate(
        [
            jnp.concatenate([outer_cols(outer_a, 0), jnp.zeros((n, w), jnp.float32)], axis=1),
            jnp.concatenate([jnp.zeros((n, w), jnp.float32), outer_cols(outer_b, 1)], axis=1),
        ],
        axis=0,
    )
    own_map = own[: 2 * n] + base
    left = jnp.where(first, own_map, cross[: 2 * n])
    right = jnp.where(first, cross[: 2 * n], own_map)
    merged_map = jnp.concatenate([left, right], axis=1).reshape(1, 8, count, 4 * w)
    own_s, cross_s = own[2 * n :], cross[2 * n :]
    second = jnp.concatenate(
        [jnp.where(first, own_s, cross_s), jnp.where(first, cross_s, own_s)], axis=1
    )
    s1 = results[2 * m :]
    y_a, y_b = -dot(own_rows[:, :f], a1y), -dot(own_rows[:, f:], b0y)

    def ordered(x, y):
        two = jnp.where(first, cols(x, 1), y)
        three = jnp.where(first, y, cols(x, 1))
        return [cols(x, 0), two, three, x[:, 2 * f :]]

    solution_first = jnp.concatenate(ordered(s1[:, :w], y_a) + ordered(s1[:, w:], y_b), axis=1)
    return (solution_first[None], second[None], merged_map)


def solution(mesh):
    return jax.shard_map(
        body,
        mesh=mesh,
        in_specs=(P("box", None, "row", None), P("box", None)),
        out_specs=(P("box", "row", None), P("box", "row", None), P("box", None, "row", None)),
        check_vma=False,
    )
```

```python
import functools

import jax
import jax.numpy as jnp
from jax import lax
from jax.experimental import pallas as pl
from jax.experimental.pallas import tpu as pltpu
from jax.sharding import PartitionSpec as P

HIGHEST = lax.Precision.HIGHEST
HIGH = lax.Precision.HIGH
BLOCK = 128
GROUP = 4


def dot(left, right, precision=HIGHEST):
    return jnp.dot(left, right, precision=precision, preferred_element_type=jnp.float32)


def dot_t(left, right):
    return lax.dot_general(
        left, right, (((0,), (0,)), ((), ())), precision=HIGHEST, preferred_element_type=jnp.float32
    )


def invert_block(blk):
    size = blk.shape[0]
    lane = lax.broadcasted_iota(jnp.int32, (1, size), 1)

    def step(g, carry):
        k = g * GROUP
        full = blk[...]
        cols = [
            jnp.take_along_axis(full, jnp.full((size, size), k + i, jnp.int32), axis=1)
            for i in range(GROUP)
        ]
        rows = [blk[pl.ds(k + i, 1), :] for i in range(GROUP)]
        wide = [jnp.broadcast_to(r, (8, size)) for r in rows]
        pivots = [
            [
                jnp.take_along_axis(wide[i], jnp.full((8, size), k + j, jnp.int32), axis=1)
                for j in range(GROUP)
            ]
            for i in range(GROUP)
        ]
        inside = (lane >= k) & (lane < k + GROUP)
        wide = [
            jnp.where(lane == k + i, 1.0, jnp.where(inside, 0.0, wide[i])) for i in range(GROUP)
        ]
        for i in range(GROUP):
            p = 1.0 / pivots[i][i]
            wide[i] = wide[i] * p
            for j in range(i + 1, GROUP):
                pivots[i][j] = pivots[i][j] * p
            for l in range(GROUP):
                if l != i:
                    f = pivots[l][i]
                    wide[l] = wide[l] - f * wide[i]
                    for j in range(i + 1, GROUP):
                        pivots[l][j] = pivots[l][j] - f * pivots[i][j]
        result = jnp.where(inside, 0.0, full)
        for i in range(GROUP):
            result = result - cols[i] * wide[i][0:1]
        blk[...] = result
        for i in range(GROUP):
            blk[pl.ds(k + i, 1), :] = wide[i][0:1]
        return carry

    lax.fori_loop(0, size // GROUP, step, 0)


def invert(mat, blk, col):
    order = mat.shape[0]
    count = order // BLOCK
    eye = (
        lax.broadcasted_iota(jnp.int32, (BLOCK, BLOCK), 0)
        == lax.broadcasted_iota(jnp.int32, (BLOCK, BLOCK), 1)
    ).astype(jnp.float32)

    def outer(j, carry):
        here = pl.ds(pl.multiple_of(j * BLOCK, BLOCK), BLOCK)
        blk[...] = mat[here, here]
        invert_block(blk)
        col[...] = mat[:, here]
        mat[:, here] = jnp.zeros((order, BLOCK), jnp.float32)
        mat[here, here] = eye
        col[here, :] = jnp.zeros((BLOCK, BLOCK), jnp.float32)
        mat[here, :] = dot(blk[...], mat[here, :])

        def inner(i, c):
            there = pl.ds(pl.multiple_of(i * BLOCK, BLOCK), BLOCK)
            mat[there, :] = mat[there, :] - dot(col[there, :], mat[here, :])
            return c

        @pl.loop(0, count)
        def _(i):
            @pl.when(i != j)
            def _():
                inner(i, 0)

        return carry

    lax.fori_loop(0, count, outer, 0)


def first_kernel(perm_ref, small_ref, inv_ref, coupled_ref, own_ref, mat, blk, col):
    f = mat.shape[0]
    count = f // BLOCK

    def block(ref, i):
        return ref[:, i * f : (i + 1) * f]

    def place(rows):
        return (
            perm_ref[rows, :] == lax.broadcasted_iota(jnp.int32, (BLOCK, f), 1)
        ).astype(jnp.float32)

    whole = (perm_ref[...] == lax.broadcasted_iota(jnp.int32, (f, f), 1)).astype(jnp.float32)

    @pl.loop(0, count)
    def _(i):
        here = pl.ds(pl.multiple_of(i * BLOCK, BLOCK), BLOCK)
        moved = dot(place(here), block(small_ref, 1))
        mat[here, :] = small_ref[here, :f] + lax.dot_general(
            moved,
            whole,
            (((1,), (1,)), ((), ())),
            precision=HIGHEST,
            preferred_element_type=jnp.float32,
        )

    invert(mat, blk, col)

    @pl.loop(0, count)
    def _(i):
        here = pl.ds(pl.multiple_of(i * BLOCK, BLOCK), BLOCK)
        inv_ref[here, :f] = mat[here, :]
        inv_ref[here, f:] = dot(mat[here, :], whole)

    @pl.loop(0, count)
    def _(i):
        there = pl.ds(pl.multiple_of(f + i * BLOCK, BLOCK), BLOCK)
        picked = (
            perm_ref[...] == lax.broadcasted_iota(jnp.int32, (f, BLOCK), 1) + i * BLOCK
        ).astype(jnp.float32)
        inv_ref[there, :] = dot_t(picked, inv_ref[:f, :])

    for h in range(2):

        @pl.loop(0, count)
        def _(i):
            here = pl.ds(pl.multiple_of(i * BLOCK, BLOCK), BLOCK)
            rows = pl.ds(pl.multiple_of(h * f + i * BLOCK, BLOCK), BLOCK)
            edge = small_ref[:, pl.ds(pl.multiple_of((2 + h) * f + i * BLOCK, BLOCK), BLOCK)]
            coupled_ref[rows, :] = -dot_t(edge, inv_ref[h * f : (h + 1) * f, :])
            for c in range(2):
                value = dot(coupled_ref[rows, c * f : (c + 1) * f], block(small_ref, 2 + c))
                if c == h:
                    value = value + small_ref[here, (4 + h) * f : (5 + h) * f]
                own_ref[rows, c * f : (c + 1) * f] = value


def second_kernel(own_ref, part_ref, lift_ref, pick_ref, out_ref, mat, blk, col):
    mat[...] = own_ref[...] + part_ref[...]
    invert(mat, blk, col)
    n = lift_ref.shape[0]
    out_ref[:n, :] = dot(lift_ref[...], mat[...])
    out_ref[n:, :] = dot(pick_ref[...], mat[...])


def flip(index, bit):
    return index + bit - 2 * bit * ((index // bit) % 2)


def plan(n, width):
    bits = []
    bit = n // 2
    while bit:
        bits.append(bit)
        bit //= 2
    tiles = width // 128
    first = tiles * 3 // 8
    second = tiles * 3 // 8 + (tiles * 3 % 8 >= 4)
    orders = [bits, bits[:-2] + [1, 2], [1, 2] + bits[:-2]]
    sizes = [first, second, tiles - first - second]
    chunks, at = [], 0
    for order, size in zip(orders, sizes):
        chunks.append((at * 128, size * 128, order))
        at += size
    return bits, chunks


def gather_kernel(n, bits, chunks, x_ref, out_ref, send_sem, recv_sem, own_sem):
    me = lax.axis_index("row")
    barrier = pltpu.get_barrier_semaphore()
    for bit in bits:
        pl.semaphore_signal(
            barrier, inc=1, device_id={"row": flip(me, bit)}, device_id_type=pl.DeviceIdType.MESH
        )
    local = pltpu.make_async_copy(x_ref, out_ref.at[me], own_sem)
    local.start()
    local.wait()
    pl.semaphore_wait(barrier, len(bits))
    pending = [[] for _ in chunks]
    sent = []
    held = [[()] for _ in chunks]
    for t in range(len(bits)):
        for c, (start, size, order) in enumerate(chunks):
            for copy in pending[c]:
                copy.wait_recv()
            pending[c] = []
            bit = order[t]
            for s in held[c]:
                slot = me
                for one in s:
                    slot = flip(slot, one)
                number = (1 << t) - 1 + len(pending[c])
                piece = out_ref.at[slot, :, pl.ds(start, size)]
                copy = pltpu.make_async_remote_copy(
                    src_ref=piece,
                    dst_ref=piece,
                    send_sem=send_sem.at[c, number],
                    recv_sem=recv_sem.at[c, number],
                    device_id={"row": flip(me, bit)},
                    device_id_type=pl.DeviceIdType.MESH,
                )
                copy.start()
                pending[c].append(copy)
                sent.append(copy)
            held[c] = held[c] + [s + (bit,) for s in held[c]]
    for c in range(len(chunks)):
        for copy in pending[c]:
            copy.wait_recv()
    for copy in sent:
        copy.wait_send()


def quick_gather(x):
    n = lax.axis_size("row")
    count, width = x.shape
    bits, chunks = plan(n, width)
    out = pl.pallas_call(
        functools.partial(gather_kernel, n, bits, chunks),
        out_shape=jax.ShapeDtypeStruct((n, count, width), jnp.float32),
        in_specs=[pl.BlockSpec(memory_space=pltpu.VMEM)],
        out_specs=pl.BlockSpec(memory_space=pltpu.VMEM),
        scratch_shapes=[
            pltpu.SemaphoreType.DMA((len(chunks), n - 1)),
            pltpu.SemaphoreType.DMA((len(chunks), n - 1)),
            pltpu.SemaphoreType.DMA,
        ],
        compiler_params=pltpu.CompilerParams(
            collective_id=0, has_side_effects=True, vmem_limit_bytes=16 * 1024 * 1024
        ),
        cost_estimate=pl.CostEstimate(
            flops=10_000_000_000, bytes_accessed=2 * n * count * width * 4, transcendentals=0
        ),
    )(x)
    return out.reshape(n * count, width)


def call(kernel, out, order, *args):
    return pl.pallas_call(
        kernel,
        out_shape=[jax.ShapeDtypeStruct(o, jnp.float32) for o in out],
        in_specs=[pl.BlockSpec(memory_space=pltpu.VMEM)] * len(args),
        out_specs=[pl.BlockSpec(memory_space=pltpu.VMEM)] * len(out),
        scratch_shapes=[
            pltpu.VMEM((order, order), jnp.float32),
            pltpu.VMEM((BLOCK, BLOCK), jnp.float32),
            pltpu.VMEM((order, BLOCK), jnp.float32),
        ],
        compiler_params=pltpu.CompilerParams(vmem_limit_bytes=40 * 1024 * 1024),
        cost_estimate=pl.CostEstimate(
            flops=order * 20_000_000, bytes_accessed=order * order * 8, transcendentals=0
        ),
    )(*args)


def body(dtn, interface_perm):
    a, b = dtn[0], dtn[1]
    count = a.shape[1]
    f = a.shape[2] // 6
    perm = interface_perm[0]
    rank = lax.axis_index("row")
    half = lax.axis_index("box") % 2
    first = half == 0

    def swap(x):
        n = lax.axis_size("box")
        return lax.ppermute(x, "box", [(i, i ^ 1) for i in range(n)])

    def gather(x):
        return lax.all_gather(x, "row", axis=0, tiled=True)

    def cols(x, face):
        return x[..., face * f : (face + 1) * f]

    def side(x):
        return jnp.where(first, cols(x, 3), cols(x, 2))

    def free(x):
        return jnp.where(first, cols(x, 2), cols(x, 3))

    def outer_cols(x, edge):
        return jnp.concatenate([cols(x, edge), free(x), cols(x, 4), cols(x, 5)], axis=-1)

    ay, by = jnp.where(first, a[3], a[2]), jnp.where(first, b[3], b[2])
    a1, b0 = a[1], b[0]
    small = quick_gather(
        jnp.concatenate(
            [cols(a1, 1), cols(b0, 0), side(a1), side(b0), side(ay), side(by)], axis=1
        )
    )
    bulk = gather(
        jnp.concatenate(
            [outer_cols(a1, 0), outer_cols(ay, 0), outer_cols(b0, 1), outer_cols(by, 1)], axis=1
        )
    )
    inv1, coupled, own_ss = call(first_kernel, [(2 * f, 2 * f)] * 3, f, perm[:, None], small)
    a1y, b0y = small[:, 2 * f : 3 * f], small[:, 3 * f : 4 * f]

    def times_side(x):
        return jnp.concatenate([dot(x[:, :f], a1y), dot(x[:, f:], b0y)], axis=1)

    part_ss = swap(own_ss)
    outer_a = jnp.concatenate(
        [a[0], jnp.where(first, a[2], a[3]), a[4], a[5]], axis=0
    )
    outer_b = jnp.concatenate(
        [b[1], jnp.where(first, b[2], b[3]), b[4], b[5]], axis=0
    )
    lift = -jnp.concatenate(
        [dot(cols(outer_a, 1), inv1[:f]), dot(cols(outer_b, 0), inv1[f:])], axis=0
    )
    n = 4 * count
    zero_n = jnp.zeros((n, f), jnp.float32)
    lift_two = times_side(lift) + jnp.concatenate(
        [
            jnp.concatenate([side(outer_a), zero_n], axis=1),
            jnp.concatenate([zero_n, side(outer_b)], axis=1),
        ],
        axis=0,
    )
    start = rank * count
    pick = (
        jnp.arange(2 * f, dtype=jnp.int32)[None, :]
        == half * f + start + jnp.arange(count, dtype=jnp.int32)[:, None]
    ).astype(jnp.float32)
    own_rows = lax.dynamic_slice(inv1, (start, 0), (count, 2 * f))
    z = -call(second_kernel, [(2 * n + count, 2 * f)], 2 * f, own_ss, part_ss, lift_two, pick)[0]
    z_part = swap(z)
    both = jnp.concatenate([z_part, z], axis=0)
    through = dot(both, coupled)
    m = 2 * n + count
    through = jnp.concatenate(
        [through[:m], through[m : m + 2 * n] + lift, through[m + 2 * n :], -own_rows], axis=0
    )
    both = jnp.concatenate([both, jnp.zeros((count, 2 * f), jnp.float32)], axis=0)
    w = 4 * f
    res_a = dot(through[:, :f], bulk[:, :w], HIGH) + dot(both[:, :f], bulk[:, w : 2 * w], HIGH)
    res_b = dot(through[:, f:], bulk[:, 2 * w : 3 * w], HIGH) + dot(both[:, f:], bulk[:, 3 * w :], HIGH)
    results = jnp.concatenate([res_a, res_b], axis=1)
    cross = swap(results[:m])
    own = results[m : 2 * m]
    base = jnp.concatenate(
        [
            jnp.concatenate([outer_cols(outer_a, 0), jnp.zeros((n, w), jnp.float32)], axis=1),
            jnp.concatenate([jnp.zeros((n, w), jnp.float32), outer_cols(outer_b, 1)], axis=1),
        ],
        axis=0,
    )
    own_map = own[: 2 * n] + base
    left = jnp.where(first, own_map, cross[: 2 * n])
    right = jnp.where(first, cross[: 2 * n], own_map)
    merged_map = jnp.concatenate([left, right], axis=1).reshape(1, 8, count, 4 * w)
    own_s, cross_s = own[2 * n :], cross[2 * n :]
    second = jnp.concatenate(
        [jnp.where(first, own_s, cross_s), jnp.where(first, cross_s, own_s)], axis=1
    )
    s1 = results[2 * m :]
    y_a, y_b = -dot(own_rows[:, :f], a1y), -dot(own_rows[:, f:], b0y)

    def ordered(x, y):
        two = jnp.where(first, cols(x, 1), y)
        three = jnp.where(first, y, cols(x, 1))
        return [cols(x, 0), two, three, x[:, 2 * f :]]

    solution_first = jnp.concatenate(ordered(s1[:, :w], y_a) + ordered(s1[:, w:], y_b), axis=1)
    return (solution_first[None], second[None], merged_map)


def solution(mesh):
    return jax.shard_map(
        body,
        mesh=mesh,
        in_specs=(P("box", None, "row", None), P("box", None)),
        out_specs=(P("box", "row", None), P("box", "row", None), P("box", None, "row", None)),
        check_vma=False,
    )
```
